32 devices in a mesh: grp: 8 (over z, y), blk: 4 (over x, core).
Axes of the slice: x: 2, y: 2, z: 4, core: 2. Of those that a mesh axis runs over, the one named last changes fastest.
Arguments:
- queries: bfloat16 [20480, 2048], P(('grp', 'blk')), may hold values from -6 to 6
- key_rows: bfloat16 [20480, 256], P(('grp', 'blk')), may hold values from -6 to 6
- value_rows: bfloat16 [20480, 256], P(('grp', 'blk')), may hold values from -6 to 6
- out_grad: bfloat16 [20480, 2048], P(('grp', 'blk')), may hold values from -12 to 12
- attn_out: bfloat16 [20480, 2048], P(('grp', 'blk')), may hold values from -6 to 6
- log_norm: float32 [20480, 16], P(('grp', 'blk')), may hold values from 4 to 7
- held_block: int32 [32], replicated, may hold values from 0 to 31, as said below
- key_block: int32 [32], replicated, may hold values from 0 to 31, as said below
Outputs:
- query_grad: bfloat16 [20480, 2048], P(('grp', 'blk'))
- key_grad: bfloat16 [20480, 256], P(('grp', 'blk'))
- value_grad: bfloat16 [20480, 256], P(('grp', 'blk'))
The draws below stay inside these ranges and needn't reach their ends.
Inputs may be any that keep to these rules, and one draw needn't show every extreme that they name: held_block is a permutation of the 32 blocks. key_block[d] <= held_block[d] for every d; a key block may be paired with many query blocks or none.
All inputs are finite; a program needn't handle non-finite values.
Results may differ from the reference program's by a relative error of at most 0.0069.
Values may be sent and summed in bfloat16 or wider, within the bound.
A program may use at most 192 MiB of HBM per device.

```python
import jax
import jax.numpy as jnp
from jax import lax

H = 16
KVH = 2
DH = 128
BLK = 640
BLOCKS = 32


def plan_pair(key):
    held = jax.random.permutation(jax.random.fold_in(key, 11), BLOCKS).astype(jnp.int32)
    raw = jax.random.randint(jax.random.fold_in(key, 12), (BLOCKS,), 0, 1048576, dtype=jnp.int32)
    chosen = raw % (held + 1)
    chosen = jnp.where(held == BLOCKS - 1, held, chosen)
    return (held, chosen.astype(jnp.int32))


def draw_held_block(key, part):
    return plan_pair(key)[0]


def draw_key_block(key, part):
    return plan_pair(key)[1]


def shard_levels(own_key, extent, split, low, high):
    level = 1.0
    for axis_at, parts in split:
        heights = jax.random.uniform(jax.random.fold_in(jax.random.fold_in(own_key, 6), axis_at), (parts,), jnp.float32, low / len(split), high / len(split))
        level = level * jnp.repeat(jnp.exp(heights), extent[axis_at] // parts).reshape((-1,) + (1,) * (len(extent) - 1 - axis_at))
    return level


def noise(rng, extent, scale, limit, pieces=(), kind=jnp.bfloat16):
    loudness = shard_levels(rng, extent, pieces, -0.22, 0.18) if pieces else 1.0
    result = jax.random.normal(rng, extent, jnp.float32) * scale * loudness
    return jnp.minimum(jnp.maximum(result, -limit), limit).astype(kind)


def setup_inputs(seed: int = 0) -> dict:
    streams_of = jax.random.split(jax.random.key(seed), 9)
    queries = noise(streams_of[0], (BLOCKS * BLK, H * DH), 1.0, 6.0, ((0, 32),))
    key_rows = noise(streams_of[1], (BLOCKS * BLK, KVH * DH), 1.0, 6.0, ((0, 32),))
    value_rows = noise(streams_of[2], (BLOCKS * BLK, KVH * DH), 1.0, 6.0, ((0, 32),))
    out_grad = noise(streams_of[3], (BLOCKS * BLK, H * DH), 2.0, 12.0, ((0, 32),))
    attn_out = noise(streams_of[4], (BLOCKS * BLK, H * DH), 1.0, 6.0, ((0, 32),))
    log_norm = jnp.clip(4.0 + 3.0 * jax.random.uniform(streams_of[5], (BLOCKS * BLK, H), jnp.float32) ** shard_levels(streams_of[5], (BLOCKS * BLK, H), ((0, 32),), -0.2, 0.2), 4.0, 7.0)
    held_block = draw_held_block(jax.random.fold_in(streams_of[8], 71), 0)
    key_block = draw_key_block(jax.random.fold_in(streams_of[8], 71), 0)
    return dict(queries=queries, key_rows=key_rows, value_rows=value_rows, out_grad=out_grad, attn_out=attn_out, log_norm=log_norm, held_block=held_block, key_block=key_block)


def pair_grads(query, dout, outs, norms, kv_rows, diag):
    rows = query.shape[0]
    group = H // KVH
    scale = DH ** -0.5
    delta = jnp.sum((dout.astype(jnp.float32) * outs.astype(jnp.float32)).reshape(rows, H, DH), axis=-1)
    row_ids = lax.broadcasted_iota(jnp.int32, (rows, rows), 0)
    col_ids = lax.broadcasted_iota(jnp.int32, (rows, rows), 1)
    keep = jnp.logical_or(jnp.logical_not(diag), col_ids <= row_ids)
    query_parts, key_parts, value_parts = [], [], []
    for head in range(KVH):
        width = group * DH
        q_head = query[:, head * width:(head + 1) * width].reshape(rows, group, DH)
        o_head = dout[:, head * width:(head + 1) * width].reshape(rows, group, DH)
        k_head = kv_rows[:, head * DH:(head + 1) * DH]
        v_head = kv_rows[:, (KVH + head) * DH:(KVH + head + 1) * DH]
        scores = jnp.einsum("igd,jd->gij", q_head.astype(jnp.float32), k_head.astype(jnp.float32)) * scale
        lse_head = jnp.transpose(norms[:, head * group:(head + 1) * group])[:, :, None]
        probs = jnp.where(keep[None], jnp.exp(scores - lse_head), 0.0)
        probs_low = probs.astype(jnp.bfloat16)
        dv_head = jnp.einsum("gij,igd->jd", probs_low.astype(jnp.float32), o_head.astype(jnp.float32))
        dprob = jnp.einsum("igd,jd->gij", o_head.astype(jnp.float32), v_head.astype(jnp.float32))
        delta_head = jnp.transpose(delta[:, head * group:(head + 1) * group])[:, :, None]
        dscore = (probs * (dprob - delta_head) * scale).astype(jnp.bfloat16)
        dq_head = jnp.einsum("gij,jd->igd", dscore.astype(jnp.float32), k_head.astype(jnp.float32))
        dk_head = jnp.einsum("gij,igd->jd", dscore.astype(jnp.float32), q_head.astype(jnp.float32))
        query_parts.append(dq_head.reshape(rows, width))
        key_parts.append(dk_head)
        value_parts.append(dv_head)
    query_grad = jnp.concatenate(query_parts, axis=1).astype(jnp.bfloat16)
    pair_term = jnp.concatenate(key_parts + value_parts, axis=1).astype(jnp.bfloat16)
    return query_grad, pair_term


def reference(queries, key_rows, value_rows, out_grad, attn_out, log_norm, held_block, key_block):
    count = held_block.shape[0]
    positions = jnp.arange(count, dtype=jnp.int32)
    holder = jnp.sum(jnp.where(held_block[None, :] == key_block[:, None], positions[None, :], 0), axis=1).astype(jnp.int32)
    q_all = queries.reshape(count, BLK, H * DH)
    d_all = out_grad.reshape(count, BLK, H * DH)
    o_all = attn_out.reshape(count, BLK, H * DH)
    n_all = log_norm.reshape(count, BLK, H)
    kv_all = jnp.concatenate([key_rows, value_rows], axis=1).reshape(count, BLK, 2 * KVH * DH)

    def one(index):
        kv_rows = kv_all[holder[index]]
        diag = held_block[index] == key_block[index]
        return pair_grads(q_all[index], d_all[index], o_all[index], n_all[index], kv_rows, diag)

    query_grad, pair_terms = lax.map(one, positions)
    summed = jax.ops.segment_sum(pair_terms.astype(jnp.float32), holder, num_segments=count)
    summed = summed.reshape(count * BLK, 2 * KVH * DH).astype(jnp.bfloat16)
    return (query_grad.reshape(count * BLK, H * DH), summed[:, :KVH * DH], summed[:, KVH * DH:])
```

```python
import functools

import jax
import jax.numpy as jnp
from jax import lax
from jax.experimental import pallas as pl
from jax.experimental.pallas import tpu as pltpu

H = 16
KVH = 2
DH = 128
GROUP = H // KVH
SCALE = DH ** (-0.5)
LOG2E = 1.4426950408889634
MESH = pl.DeviceIdType.MESH


def chunks_of(rows, width):
    return [(at, min(width, rows - at)) for at in range(0, rows, width)]


def plan_kernel(n, held_ref, key_ref, plan_ref, inv, count):
    def zero(e, c):
        count[e] = 0
        return c

    def invert(e, c):
        inv[held_ref[e]] = e
        return c

    def hold(d, c):
        e = inv[key_ref[d]]
        plan_ref[d] = e
        count[e] = count[e] + 1
        return c

    def prefix(e, at):
        many = count[e]
        count[e] = at
        plan_ref[3 * n + e] = jnp.maximum(at + many - 1, 0)
        plan_ref[4 * n + e] = jnp.minimum(many, 1)
        return at + many

    def place(d, c):
        e = plan_ref[d]
        at = count[e]
        plan_ref[n + at] = d
        plan_ref[2 * n + at] = inv[e]
        inv[e] = 1
        count[e] = at + 1
        return c

    def clear(e, c):
        inv[e] = 0
        return c

    lax.fori_loop(0, n, zero, 0)
    lax.fori_loop(0, n, invert, 0)
    lax.fori_loop(0, n, hold, 0)
    lax.fori_loop(0, n, prefix, 0)
    lax.fori_loop(0, n, clear, 0)
    lax.fori_loop(0, n, place, 0)


def make_plan(n, held_block, key_block):
    return pl.pallas_call(
        functools.partial(plan_kernel, n),
        out_shape=jax.ShapeDtypeStruct((5 * n,), jnp.int32),
        in_specs=[pl.BlockSpec(memory_space=pltpu.SMEM)] * 2,
        out_specs=pl.BlockSpec(memory_space=pltpu.SMEM),
        scratch_shapes=[pltpu.SMEM((n,), jnp.int32), pltpu.SMEM((n,), jnp.int32)],
    )(held_block, key_block)


def own_place():
    return lax.axis_index("grp") * lax.axis_size("blk") + lax.axis_index("blk")


def meet_all(n, n_blk, me):
    barrier = pltpu.get_barrier_semaphore()

    def greet(k, c):
        t = lax.rem(me + k, n)
        pl.semaphore_signal(
            barrier, inc=1, device_id=(t // n_blk, lax.rem(t, n_blk)), device_id_type=MESH
        )
        return c

    lax.fori_loop(1, n, greet, 0)
    pl.semaphore_wait(barrier, n - 1)


def start_exchange(n, n_blk, me, src, dst, send_sem, recv_sem):
    def push(k, c):
        t = lax.rem(me + k, n)
        pltpu.make_async_remote_copy(
            src_ref=src.at[t],
            dst_ref=dst.at[me],
            send_sem=send_sem,
            recv_sem=recv_sem,
            device_id=(t // n_blk, lax.rem(t, n_blk)),
            device_id_type=MESH,
        ).start()
        return c

    lax.fori_loop(1, n, push, 0)


def wait_bytes(n, ref, sem):
    part = ref.at[pl.ds(0, n - 1)]
    pltpu.make_async_copy(part, part, sem).wait()


def fetch_kernel(n, n_blk, plan_ref, kv_ref, out_ref, held, picked, sems):
    me = own_place()
    meet_all(n, n_blk, me)
    start_exchange(n, n_blk, me, kv_ref, held, sems.at[0], sems.at[1])
    held[me] = kv_ref[me]
    wait_bytes(n, held, sems.at[1])

    def pick(d, c):
        picked[d] = held[plan_ref[d]]
        return c

    lax.fori_loop(0, n, pick, 0)
    start_exchange(n, n_blk, me, picked, out_ref, sems.at[2], sems.at[3])
    out_ref[me] = picked[me]
    wait_bytes(n, kv_ref, sems.at[0])
    wait_bytes(n, picked, sems.at[2])
    wait_bytes(n, out_ref, sems.at[3])


def return_kernel(n, n_blk, plan_ref, pair_ref, out_ref, terms, sums, picked, sems):
    me = own_place()
    meet_all(n, n_blk, me)
    start_exchange(n, n_blk, me, pair_ref, terms, sems.at[0], sems.at[1])
    terms[me] = pair_ref[me]
    wait_bytes(n, terms, sems.at[1])

    def add(k, total):
        term = terms[plan_ref[n + k]].astype(jnp.float32)
        total = jnp.where(plan_ref[2 * n + k] == 1, total, 0.0) + term
        sums[k] = total
        return total

    lax.fori_loop(0, n, add, jnp.zeros(sums.shape[1:], jnp.float32))

    def pick(e, c):
        total = sums[plan_ref[3 * n + e]]
        picked[e] = jnp.where(plan_ref[4 * n + e] == 1, total, 0.0).astype(jnp.bfloat16)
        return c

    lax.fori_loop(0, n, pick, 0)
    start_exchange(n, n_blk, me, picked, out_ref, sems.at[2], sems.at[3])
    out_ref[me] = picked[me]
    wait_bytes(n, pair_ref, sems.at[0])
    wait_bytes(n, picked, sems.at[2])
    wait_bytes(n, out_ref, sems.at[3])


def exchange_call(kernel, n, n_blk, plan, pieces, scratch, collective_id):
    vmem = pl.BlockSpec(memory_space=pltpu.VMEM)
    return pl.pallas_call(
        functools.partial(kernel, n, n_blk),
        out_shape=jax.ShapeDtypeStruct(pieces.shape, jnp.bfloat16),
        in_specs=[pl.BlockSpec(memory_space=pltpu.SMEM), vmem],
        out_specs=vmem,
        scratch_shapes=scratch + [pltpu.SemaphoreType.DMA((4,))],
        compiler_params=pltpu.CompilerParams(collective_id=collective_id, has_side_effects=True),
    )(plan, pieces)


NT = (((1,), (1,)), ((), ()))
TN = (((0,), (0,)), ((), ()))


def pair_kernel(width, diag_ref, lse_ref, q_ref, do_ref, o_ref, k_ref, v_ref, dq_ref, pair_ref, dk_acc, dv_acc):
    head = pl.program_id(0)
    rows = q_ref.shape[0]
    step = lax.rem(head, GROUP)

    @pl.when(step == 0)
    def _():
        dk_acc[...] = jnp.zeros_like(dk_acc)
        dv_acc[...] = jnp.zeros_like(dv_acc)

    def body(diag):
        for at, w in chunks_of(rows, width):
            keys = min(rows, at + w) if diag else rows
            q = q_ref[at : at + w, :]
            do = do_ref[at : at + w, :]
            o = o_ref[at : at + w, :]
            k = k_ref[0, :keys, :]
            v = v_ref[0, :keys, :]
            lse = lse_ref[0, :, at : at + w] * LOG2E
            prod = do.astype(jnp.float32) * o.astype(jnp.float32)
            delta = jnp.sum(jnp.transpose(prod), axis=0, keepdims=True)
            s = lax.dot_general(k, q, NT, preferred_element_type=jnp.float32)
            p = jnp.exp2(s * (SCALE * LOG2E) - lse)
            if diag:
                j = lax.broadcasted_iota(jnp.int32, p.shape, 0)
                i = lax.broadcasted_iota(jnp.int32, p.shape, 1) + at
                p = jnp.where(j <= i, p, 0.0)
            dp = lax.dot_general(v, do, NT, preferred_element_type=jnp.float32)
            ds = (p * (dp - delta)).astype(jnp.bfloat16)
            dv_acc[:keys, :] += jnp.dot(
                p.astype(jnp.bfloat16), do, preferred_element_type=jnp.float32
            )
            dk_acc[:keys, :] += jnp.dot(ds, q, preferred_element_type=jnp.float32)
            dq = lax.dot_general(ds, k, TN, preferred_element_type=jnp.float32)
            dq_ref[at : at + w, :] = (dq * SCALE).astype(jnp.bfloat16)

    @pl.when(diag_ref[0] == 1)
    def _():
        body(True)

    @pl.when(diag_ref[0] == 0)
    def _():
        body(False)

    @pl.when(step == GROUP - 1)
    def _():
        pair_ref[0, 0] = (dk_acc[...] * SCALE).astype(jnp.bfloat16)
        pair_ref[1, 0] = dv_acc[...].astype(jnp.bfloat16)


def pair_grads(queries, out_grad, attn_out, lse, kv, diag, width=256):
    rows = queries.shape[0]
    col = pl.BlockSpec((rows, DH), lambda h: (0, h))
    return pl.pallas_call(
        functools.partial(pair_kernel, width),
        out_shape=(
            jax.ShapeDtypeStruct((rows, H * DH), jnp.bfloat16),
            jax.ShapeDtypeStruct((2, KVH, rows, DH), jnp.bfloat16),
        ),
        grid=(H,),
        in_specs=[
            pl.BlockSpec(memory_space=pltpu.SMEM),
            pl.BlockSpec((1, 1, rows), lambda h: (h, 0, 0)),
            col,
            col,
            col,
            pl.BlockSpec((1, rows, DH), lambda h: (h // GROUP, 0, 0)),
            pl.BlockSpec((1, rows, DH), lambda h: (KVH + h // GROUP, 0, 0)),
        ],
        out_specs=(col, pl.BlockSpec((2, 1, rows, DH), lambda h: (0, h // GROUP, 0, 0))),
        scratch_shapes=[pltpu.VMEM((rows, DH), jnp.float32)] * 2,
        compiler_params=pltpu.CompilerParams(dimension_semantics=("arbitrary",)),
    )(diag, lse, queries, out_grad, attn_out, kv, kv)


def split_heads(rows_array):
    return [rows_array[:, c * DH : (c + 1) * DH] for c in range(KVH)]


def per_device(queries, key_rows, value_rows, out_grad, attn_out, log_norm, held_block, key_block):
    n_blk = lax.axis_size("blk")
    n = lax.axis_size("grp") * n_blk
    rows = queries.shape[0]
    me = own_place()
    part = 2 * KVH * rows // n
    piece = (n, part, DH)
    diag = (
        lax.dynamic_slice_in_dim(held_block, me, 1) == lax.dynamic_slice_in_dim(key_block, me, 1)
    ).astype(jnp.int32)
    plan = make_plan(n, held_block, key_block)
    kv_own = jnp.stack(split_heads(key_rows) + split_heads(value_rows)).reshape(piece)
    buf = pltpu.VMEM(piece, jnp.bfloat16)
    kv = exchange_call(fetch_kernel, n, n_blk, plan, kv_own, [buf, buf], 0)
    kv = kv.reshape(2 * KVH, rows, DH)
    lse = jnp.transpose(log_norm)[:, None, :]
    query_grad, pair = pair_grads(queries, out_grad, attn_out, lse, kv, diag)
    grads = exchange_call(
        return_kernel, n, n_blk, plan, pair.reshape(piece),
        [buf, pltpu.VMEM(piece, jnp.float32), buf], 1,
    )
    grads = grads.reshape(2, KVH, rows, DH)
    key_grad = jnp.concatenate([grads[0, c] for c in range(KVH)], axis=1)
    value_grad = jnp.concatenate([grads[1, c] for c in range(KVH)], axis=1)
    return query_grad, key_grad, value_grad


def solution(mesh):
    row = jax.sharding.PartitionSpec(("grp", "blk"), None)
    flat = jax.sharding.PartitionSpec()
    return jax.shard_map(
        per_device,
        mesh=mesh,
        in_specs=(row, row, row, row, row, row, flat, flat),
        out_specs=(row, row, row),
        check_vma=False,
    )
```

```python
import functools

import jax
import jax.numpy as jnp
from jax import lax
from jax.experimental import pallas as pl
from jax.experimental.pallas import tpu as pltpu

H = 16
KVH = 2
DH = 128
GROUP = H // KVH
SCALE = DH ** (-0.5)
LOG2E = 1.4426950408889634
MESH = pl.DeviceIdType.MESH


def chunks_of(rows, width):
    return [(at, min(width, rows - at)) for at in range(0, rows, width)]


def plan_kernel(n, held_ref, key_ref, plan_ref, inv, count):
    def zero(e, c):
        count[e] = 0
        return c

    def invert(e, c):
        inv[held_ref[e]] = e
        return c

    def hold(d, c):
        e = inv[key_ref[d]]
        plan_ref[d] = e
        count[e] = count[e] + 1
        return c

    def prefix(e, at):
        many = count[e]
        count[e] = at
        plan_ref[3 * n + e] = jnp.maximum(at + many - 1, 0)
        plan_ref[4 * n + e] = jnp.minimum(many, 1)
        return at + many

    def place(d, c):
        e = plan_ref[d]
        at = count[e]
        plan_ref[n + at] = d
        plan_ref[2 * n + at] = inv[e]
        inv[e] = 1
        count[e] = at + 1
        return c

    def clear(e, c):
        inv[e] = 0
        return c

    me = own_place()
    plan_ref[5 * n] = jnp.where(held_ref[me] == key_ref[me], 1, 0)
    lax.fori_loop(0, n, zero, 0)
    lax.fori_loop(0, n, invert, 0)
    lax.fori_loop(0, n, hold, 0)
    lax.fori_loop(0, n, prefix, 0)
    lax.fori_loop(0, n, clear, 0)
    lax.fori_loop(0, n, place, 0)


def make_plan(n, held_block, key_block):
    return pl.pallas_call(
        functools.partial(plan_kernel, n),
        out_shape=jax.ShapeDtypeStruct((5 * n + 1,), jnp.int32),
        in_specs=[pl.BlockSpec(memory_space=pltpu.SMEM)] * 2,
        out_specs=pl.BlockSpec(memory_space=pltpu.SMEM),
        scratch_shapes=[pltpu.SMEM((n,), jnp.int32), pltpu.SMEM((n,), jnp.int32)],
    )(held_block, key_block)


def own_place():
    return lax.axis_index("grp") * lax.axis_size("blk") + lax.axis_index("blk")


NT = (((1,), (1,)), ((), ()))
TN = (((0,), (0,)), ((), ()))
FAR = 1e30


def fused_kernel(
    n, n_blk, m, width, plan_ref, kv_ref, lse_ref, q_hbm, do_hbm, o_hbm,
    dq_hbm, out_ref,
    q_ref, do_ref, o_ref, dq_ref, lse3, delta3, held, picked, kv, pair, terms, sums, sent,
    dk_acc, dv_acc, sems, local_sems,
):
    rows = q_ref.shape[0]
    half = m // 2
    me = own_place()
    kind = lax.rem(me, 2)
    slot = kind * half + me // 2
    relay = me < m
    fetch_in, fetch_out, return_in, return_out = [sems.at[i] for i in range(4)]
    kv_out, kv_in, pair_out, grad_in = [(sems.at[i], sems.at[i + 1]) for i in range(4, 12, 2)]
    place = lambda t: (t // n_blk, lax.rem(t, n_blk))

    loads = [
        pltpu.make_async_copy(src, dst, local_sems.at[i])
        for i, (src, dst) in enumerate(((do_hbm, do_ref), (o_hbm, o_ref), (q_hbm, q_ref)))
    ]
    barrier = pltpu.get_barrier_semaphore()

    def greet(k, c):
        pl.semaphore_signal(
            barrier, inc=1, device_id=place(lax.rem(me + k, n)), device_id_type=MESH
        )
        return c

    lax.fori_loop(1, n, greet, 0)
    for load in loads:
        load.start()
    pl.semaphore_wait(barrier, n - 1)

    def to_relays(c, src, dst, send_sem, recv_sem):
        def push(k, carry):
            at = lax.rem(me // 2 + k, half)
            t = 2 * at + c

            @pl.when(t != me)
            def _():
                pltpu.make_async_remote_copy(
                    src_ref=src.at[c * half + at], dst_ref=dst.at[me],
                    send_sem=send_sem, recv_sem=recv_sem,
                    device_id=place(t), device_id_type=MESH,
                ).start()

            return carry

        lax.fori_loop(0, half, push, 0)

        @pl.when(jnp.logical_and(relay, kind == c))
        def _():
            dst[me] = src[slot]

    def from_relay(src, dst, send_sem, recv_sem):
        def push(k, carry):
            t = lax.rem(me + k, n)
            pltpu.make_async_remote_copy(
                src_ref=src.at[t], dst_ref=dst.at[slot],
                send_sem=send_sem, recv_sem=recv_sem,
                device_id=place(t), device_id_type=MESH,
            ).start()
            return carry

        lax.fori_loop(1, n, push, 0)
        dst[slot] = src[me]

    def wait(ref, count, sem):
        part = ref.at[pl.ds(0, count)]
        pltpu.make_async_copy(part, part, sem).wait()

    def wait_pieces(c, ref, sem):
        mine = jnp.logical_and(relay, kind == c)

        @pl.when(mine)
        def _():
            wait(ref, half - 1, sem)

        @pl.when(jnp.logical_not(mine))
        def _():
            wait(ref, half, sem)

    def on_relay(c, work):
        @pl.when(jnp.logical_and(relay, kind == c))
        def _():
            work(c)

    def deliver(c):
        wait(held, n - 1, fetch_in)

        def pick(d, carry):
            picked[d] = held[plan_ref[d]]
            return carry

        lax.fori_loop(0, n, pick, 0)
        from_relay(picked, kv, fetch_out, kv_in[c])

    def settle(c):
        wait(terms, n - 1, return_in)

        def add(k, total):
            term = terms[plan_ref[n + k]].astype(jnp.float32)
            total = jnp.where(plan_ref[2 * n + k] == 1, total, 0.0) + term
            sums[k] = total
            return total

        lax.fori_loop(0, n, add, jnp.zeros(sums.shape[1:], jnp.float32))

        def pick(e, carry):
            total = sums[plan_ref[3 * n + e]]
            sent[e] = jnp.where(plan_ref[4 * n + e] == 1, total, 0.0).astype(jnp.bfloat16)
            return carry

        lax.fori_loop(0, n, pick, 0)
        from_relay(sent, out_ref, return_out, grad_in[c])

    def heads(c, first, last):
        diag = plan_ref[5 * n]
        slack = rows * (1 - diag)

        def one(h, carry):
            col = pl.ds(pl.multiple_of(h * DH, DH), DH)
            k = kv[c * half : c * half + half // 2].reshape(rows, DH)
            v = kv[c * half + half // 2 : (c + 1) * half].reshape(rows, DH)
            dk, dv = dk_acc[...], dv_acc[...]
            for at, w in chunks_of(rows, width):
                q = q_ref[at : at + w, col]
                do = do_ref[at : at + w, col]
                lse = lse3[h, :, at : at + w]
                delta = delta3[h, :, at : at + w]
                s = lax.dot_general(k, q, NT, preferred_element_type=jnp.float32)
                s = s * (SCALE * LOG2E)
                parts = []
                if at:
                    parts.append(jnp.exp2(s[:at] - lse))
                square = jnp.exp2(s[at : at + w] - lse)
                j = lax.broadcasted_iota(jnp.int32, square.shape, 0)
                i = lax.broadcasted_iota(jnp.int32, square.shape, 1)
                parts.append(jnp.where(j - i <= slack, square, 0.0))
                if at + w < rows:
                    parts.append(jnp.exp2(s[at + w :] - jnp.where(diag == 1, FAR, lse)))
                p = jnp.concatenate(parts, axis=0)
                dp = lax.dot_general(v, do, NT, preferred_element_type=jnp.float32)
                ds = (p * (dp - delta)).astype(jnp.bfloat16)
                dv = dv + jnp.dot(p.astype(jnp.bfloat16), do, preferred_element_type=jnp.float32)
                dk = dk + jnp.dot(ds, q, preferred_element_type=jnp.float32)
                dq = lax.dot_general(ds, k, TN, preferred_element_type=jnp.float32)
                dq_ref[at : at + w, col] = (dq * SCALE).astype(jnp.bfloat16)
            dk_acc[...] = dk
            dv_acc[...] = dv
            return carry

        lax.fori_loop(first, last, one, 0)

    def clear():
        dk_acc[...] = jnp.zeros_like(dk_acc)
        dv_acc[...] = jnp.zeros_like(dv_acc)

    def store_pair(c):
        shape = (half // 2,) + pair.shape[1:]
        pair[c * half : c * half + half // 2] = (
            (dk_acc[...] * SCALE).astype(jnp.bfloat16).reshape(shape)
        )
        pair[c * half + half // 2 : (c + 1) * half] = (
            dv_acc[...].astype(jnp.bfloat16).reshape(shape)
        )

    to_relays(0, kv_ref, held, kv_out[0], fetch_in)
    for h in range(H):
        lse3[h] = lse_ref[h : h + 1, :] * LOG2E
    loads[0].wait()
    loads[1].wait()

    def make_delta(h, carry):
        col = pl.ds(pl.multiple_of(h * DH, DH), DH)
        prod = do_ref[:, col].astype(jnp.float32) * o_ref[:, col].astype(jnp.float32)
        delta3[h] = jnp.sum(jnp.transpose(prod), axis=0, keepdims=True)
        return carry

    lax.fori_loop(0, H, make_delta, 0)
    loads[2].wait()
    first = jnp.logical_and(relay, kind == 0)

    @pl.when(first)
    def _():
        deliver(0)
        to_relays(1, kv_ref, held, kv_out[1], fetch_in)

    wait_pieces(0, kv, kv_in[0])

    @pl.when(jnp.logical_not(first))
    def _():
        to_relays(1, kv_ref, held, kv_out[1], fetch_in)

    clear()
    heads(0, 0, GROUP // 2)
    on_relay(1, deliver)
    heads(0, GROUP // 2, GROUP)
    store_pair(0)
    to_relays(0, pair, terms, pair_out[0], return_in)
    wait_pieces(1, kv, kv_in[1])
    clear()
    heads(1, GROUP, GROUP + GROUP // 2)
    on_relay(0, settle)
    heads(1, GROUP + GROUP // 2, H)
    store_pair(1)
    to_relays(1, pair, terms, pair_out[1], return_in)
    save = pltpu.make_async_copy(dq_ref, dq_hbm, local_sems.at[0])
    save.start()
    on_relay(1, settle)
    for c in range(KVH):
        wait_pieces(c, kv_ref, kv_out[c])
        wait_pieces(c, pair, pair_out[c])
        wait_pieces(c, out_ref, grad_in[c])

    @pl.when(relay)
    def _():
        wait(picked, n - 1, fetch_out)
        wait(sent, n - 1, return_out)

    save.wait()


def relay_count(n, rows):
    fits = [
        m for m in range(4, n + 1, 4)
        if 4 * rows % m == 0 and (4 * rows // m) % 16 == 0 and rows % (4 * rows // m) == 0
    ]
    return max(fits)


def per_device(queries, key_rows, value_rows, out_grad, attn_out, log_norm, held_block, key_block):
    n_blk = lax.axis_size("blk")
    n = lax.axis_size("grp") * n_blk
    rows = queries.shape[0]
    m = relay_count(n, rows)
    part = 2 * KVH * rows // m
    plan = make_plan(n, held_block, key_block)
    cut = lambda x, c: x[:, c * DH : (c + 1) * DH]
    kv_own = jnp.stack([cut(x, c) for c in range(KVH) for x in (key_rows, value_rows)])
    lse = jnp.transpose(log_norm)
    vmem = pl.BlockSpec(memory_space=pltpu.VMEM)
    hbm = pl.BlockSpec(memory_space=pl.ANY)
    wide = pltpu.VMEM((rows, H * DH), jnp.bfloat16)
    line = pltpu.VMEM((H, 1, rows), jnp.float32)
    by_device = pltpu.VMEM((n, part, DH), jnp.bfloat16)
    by_slot = pltpu.VMEM((m, part, DH), jnp.bfloat16)
    acc = pltpu.VMEM((rows, DH), jnp.float32)
    query_grad, grads = pl.pallas_call(
        functools.partial(fused_kernel, n, n_blk, m, 256),
        out_shape=(
            jax.ShapeDtypeStruct((rows, H * DH), jnp.bfloat16),
            jax.ShapeDtypeStruct((m, part, DH), jnp.bfloat16),
        ),
        in_specs=[pl.BlockSpec(memory_space=pltpu.SMEM), vmem, vmem, hbm, hbm, hbm],
        out_specs=(hbm, vmem),
        scratch_shapes=[
            wide, wide, wide, wide, line, line,
            by_device, by_device, by_slot, by_slot, by_device,
            pltpu.VMEM((n, part, DH), jnp.float32), by_device,
            acc, acc, pltpu.SemaphoreType.DMA((12,)), pltpu.SemaphoreType.DMA((3,)),
        ],
        compiler_params=pltpu.CompilerParams(collective_id=0, has_side_effects=True),
    )(plan, kv_own.reshape(m, part, DH), lse, queries, out_grad, attn_out)
    grads = grads.reshape(KVH, 2, rows, DH)
    key_grad = jnp.concatenate([grads[c, 0] for c in range(KVH)], axis=1)
    value_grad = jnp.concatenate([grads[c, 1] for c in range(KVH)], axis=1)
    return query_grad, key_grad, value_grad


def solution(mesh):
    row = jax.sharding.PartitionSpec(("grp", "blk"), None)
    flat = jax.sharding.PartitionSpec()
    return jax.shard_map(
        per_device,
        mesh=mesh,
        in_specs=(row, row, row, row, row, row, flat, flat),
        out_specs=(row, row, row),
        check_vma=False,
    )
```

```python
import functools

import jax
import jax.numpy as jnp
from jax import lax
from jax.experimental import pallas as pl
from jax.experimental.pallas import tpu as pltpu

H = 16
KVH = 2
DH = 128
GROUP = H // KVH
SCALE = DH ** (-0.5)
LOG2E = 1.4426950408889634
MESH = pl.DeviceIdType.MESH


def chunks_of(rows, width):
    return [(at, min(width, rows - at)) for at in range(0, rows, width)]


def own_place():
    return lax.axis_index("grp") * lax.axis_size("blk") + lax.axis_index("blk")


NT = (((1,), (1,)), ((), ()))
TN = (((0,), (0,)), ((), ()))
FAR = 1e30


def fused_kernel(
    n, n_blk, m, width, held_ref, key_ref, k_ref, v_ref, lse_ref, q_hbm, do_hbm, o_hbm,
    dq_hbm, dk_ref, dv_ref,
    q_ref, do_ref, o_ref, dq_ref, lse3, delta3, held, picked, kv, pair, terms, sums, sent,
    dk_acc, dv_acc, holder, before, last_of, sems, local_sems,
):
    rows = q_ref.shape[0]
    half = m // 2
    me = own_place()
    kind = lax.rem(me, 2)
    slot = kind * half + me // 2
    part = held.shape[1]
    block_row = pl.multiple_of(lax.rem(me // 2, half // 2) * part, part)
    of_keys = me // 2 < half // 2
    relay = me < m
    fetch_in, fetch_out, return_in, return_out = [sems.at[i] for i in range(4)]
    kv_out, kv_in, pair_out, grad_in = [(sems.at[i], sems.at[i + 1]) for i in range(4, 12, 2)]
    place = lambda t: (t // n_blk, lax.rem(t, n_blk))

    loads = [
        pltpu.make_async_copy(src, dst, local_sems.at[i])
        for i, (src, dst) in enumerate(((do_hbm, do_ref), (o_hbm, o_ref), (q_hbm, q_ref)))
    ]
    barrier = pltpu.get_barrier_semaphore()

    def greet(k, c):
        pl.semaphore_signal(
            barrier, inc=1, device_id=place(lax.rem(me + k, n)), device_id_type=MESH
        )
        return c

    lax.fori_loop(1, n, greet, 0)
    for load in loads:
        load.start()
    pl.semaphore_wait(barrier, n - 1)

    def to_relays(c, src, dst, send_sem, recv_sem):
        def push(k, carry):
            at = lax.rem(me // 2 + k, half)
            t = 2 * at + c

            @pl.when(t != me)
            def _():
                pltpu.make_async_remote_copy(
                    src_ref=src.at[c * half + at], dst_ref=dst.at[me],
                    send_sem=send_sem, recv_sem=recv_sem,
                    device_id=place(t), device_id_type=MESH,
                ).start()

            return carry

        lax.fori_loop(0, half, push, 0)

        @pl.when(jnp.logical_and(relay, kind == c))
        def _():
            dst[me] = src[slot]

    def send_blocks(c):
        cols = slice(c * DH, (c + 1) * DH)

        def push(k, carry):
            i = lax.rem(me // 2 + k, half // 2)
            row = pl.multiple_of(i * part, part)
            for src, at in ((k_ref, i), (v_ref, half // 2 + i)):
                t = 2 * at + c

                @pl.when(t != me)
                def _():
                    pltpu.make_async_remote_copy(
                        src_ref=src.at[pl.ds(row, part), cols], dst_ref=held.at[me],
                        send_sem=kv_out[c], recv_sem=fetch_in,
                        device_id=place(t), device_id_type=MESH,
                    ).start()

            return carry

        lax.fori_loop(0, half // 2, push, 0)
        mine = jnp.logical_and(relay, kind == c)

        @pl.when(jnp.logical_and(mine, of_keys))
        def _():
            held[me] = k_ref[pl.ds(block_row, part), cols]

        @pl.when(jnp.logical_and(mine, jnp.logical_not(of_keys)))
        def _():
            held[me] = v_ref[pl.ds(block_row, part), cols]

    def from_relay(src, dst, send_sem, recv_sem):
        def push(k, carry):
            t = lax.rem(me + k, n)
            pltpu.make_async_remote_copy(
                src_ref=src.at[t], dst_ref=dst,
                send_sem=send_sem, recv_sem=recv_sem,
                device_id=place(t), device_id_type=MESH,
            ).start()
            return carry

        lax.fori_loop(1, n, push, 0)

    def wait(ref, count, sem):
        part = ref.at[pl.ds(0, count)]
        pltpu.make_async_copy(part, part, sem).wait()

    def wait_pieces(c, ref, sem):
        mine = jnp.logical_and(relay, kind == c)

        @pl.when(mine)
        def _():
            wait(ref, half - 1, sem)

        @pl.when(jnp.logical_not(mine))
        def _():
            wait(ref, half, sem)

    def on_relay(c, work):
        @pl.when(jnp.logical_and(relay, kind == c))
        def _():
            work(c)

    def deliver(c):
        wait(held, n - 1, fetch_in)

        def pick(d, carry):
            picked[d] = held[holder[d]]
            return carry

        lax.fori_loop(0, n, pick, 0)
        from_relay(picked, kv.at[slot], fetch_out, kv_in[c])
        kv[slot] = picked[me]

    def settle(c):
        wait(terms, n - 1, return_in)

        def add(d, carry):
            earlier = before[d]
            total = jnp.where(earlier >= 0, sums[jnp.maximum(earlier, 0)], 0.0)
            sums[d] = total + terms[d].astype(jnp.float32)
            return carry

        sums[0] = jnp.zeros_like(sums[0])
        lax.fori_loop(0, n, add, 0)

        def pick(e, carry):
            d = last_of[e]
            total = jnp.where(d >= 0, sums[jnp.maximum(d, 0)], 0.0)
            sent[e] = total.astype(jnp.bfloat16)
            return carry

        lax.fori_loop(0, n, pick, 0)
        cols = slice(c * DH, (c + 1) * DH)
        for dst, mine in ((dk_ref, of_keys), (dv_ref, jnp.logical_not(of_keys))):

            @pl.when(mine)
            def _():
                spot = dst.at[pl.ds(block_row, part), cols]
                from_relay(sent, spot, return_out, grad_in[c])
                dst[pl.ds(block_row, part), cols] = sent[me]

    def heads(c, first, last):
        diag = jnp.where(held_ref[me] == key_ref[me], 1, 0)
        slack = rows * (1 - diag)

        def one(h, carry):
            col = pl.ds(pl.multiple_of(h * DH, DH), DH)
            k = kv[c * half : c * half + half // 2].reshape(rows, DH)
            v = kv[c * half + half // 2 : (c + 1) * half].reshape(rows, DH)
            dk, dv = dk_acc[...], dv_acc[...]
            for at, w in chunks_of(rows, width):
                q = q_ref[at : at + w, col]
                do = do_ref[at : at + w, col]
                lse = lse3[h, :, at : at + w]
                delta = delta3[h, :, at : at + w]
                s = lax.dot_general(k, q, NT, preferred_element_type=jnp.float32)
                s = s * (SCALE * LOG2E)
                parts = []
                if at:
                    parts.append(jnp.exp2(s[:at] - lse))
                square = jnp.exp2(s[at : at + w] - lse)
                j = lax.broadcasted_iota(jnp.int32, square.shape, 0)
                i = lax.broadcasted_iota(jnp.int32, square.shape, 1)
                parts.append(jnp.where(j - i <= slack, square, 0.0))
                if at + w < rows:
                    parts.append(jnp.exp2(s[at + w :] - jnp.where(diag == 1, FAR, lse)))
                p = jnp.concatenate(parts, axis=0)
                dp = lax.dot_general(v, do, NT, preferred_element_type=jnp.float32)
                ds = (p * (dp - delta)).astype(jnp.bfloat16)
                dv = dv + jnp.dot(p.astype(jnp.bfloat16), do, preferred_element_type=jnp.float32)
                dk = dk + jnp.dot(ds, q, preferred_element_type=jnp.float32)
                dq = lax.dot_general(ds, k, TN, preferred_element_type=jnp.float32)
                dq_ref[at : at + w, col] = (dq * SCALE).astype(jnp.bfloat16)
            dk_acc[...] = dk
            dv_acc[...] = dv
            return carry

        lax.fori_loop(first, last, one, 0)

    def clear():
        dk_acc[...] = jnp.zeros_like(dk_acc)
        dv_acc[...] = jnp.zeros_like(dv_acc)

    def store_pair(c):
        shape = (half // 2,) + pair.shape[1:]
        pair[c * half : c * half + half // 2] = (
            (dk_acc[...] * SCALE).astype(jnp.bfloat16).reshape(shape)
        )
        pair[c * half + half // 2 : (c + 1) * half] = (
            dv_acc[...].astype(jnp.bfloat16).reshape(shape)
        )

    send_blocks(0)

    def find(count, test, none):
        def step(i, found):
            return jnp.where(test(i), i, found)

        return lax.fori_loop(0, count, step, none, unroll=8)

    def plan_holder(d, carry):
        block = key_ref[d]
        holder[d] = find(n, lambda e: held_ref[e] == block, 0)
        return carry

    def plan_sums(d, carry):
        own = holder[d]
        before[d] = find(n, lambda i: jnp.logical_and(holder[i] == own, i < d), -1)
        last_of[d] = find(n, lambda i: holder[i] == d, -1)
        return carry

    lax.fori_loop(0, n, plan_holder, 0)
    lax.fori_loop(0, n, plan_sums, 0)
    for h in range(H):
        lse3[h] = lse_ref[h : h + 1, :] * LOG2E
    loads[0].wait()
    loads[1].wait()

    def make_delta(h, carry):
        col = pl.ds(pl.multiple_of(h * DH, DH), DH)
        prod = do_ref[:, col].astype(jnp.float32) * o_ref[:, col].astype(jnp.float32)
        delta3[h] = jnp.sum(jnp.transpose(prod), axis=0, keepdims=True)
        return carry

    lax.fori_loop(0, H, make_delta, 0)
    loads[2].wait()
    first = jnp.logical_and(relay, kind == 0)

    @pl.when(first)
    def _():
        deliver(0)
        send_blocks(1)

    wait_pieces(0, kv, kv_in[0])

    @pl.when(jnp.logical_not(first))
    def _():
        send_blocks(1)

    clear()
    heads(0, 0, GROUP // 2)
    on_relay(1, deliver)
    heads(0, GROUP // 2, GROUP)
    store_pair(0)
    to_relays(0, pair, terms, pair_out[0], return_in)
    wait_pieces(1, kv, kv_in[1])
    clear()
    heads(1, GROUP, GROUP + GROUP // 2)
    on_relay(0, settle)
    heads(1, GROUP + GROUP // 2, H)
    store_pair(1)
    to_relays(1, pair, terms, pair_out[1], return_in)
    save = pltpu.make_async_copy(dq_ref, dq_hbm, local_sems.at[0])
    save.start()
    on_relay(1, settle)
    for c in range(KVH):
        wait_pieces(c, kv, kv_out[c])
        wait_pieces(c, pair, pair_out[c])
        wait_pieces(c, pair, grad_in[c])

    @pl.when(relay)
    def _():
        wait(picked, n - 1, fetch_out)
        wait(sent, n - 1, return_out)

    save.wait()


def relay_count(n, rows):
    fits = [
        m for m in range(4, n + 1, 4)
        if 4 * rows % m == 0 and (4 * rows // m) % 16 == 0 and rows % (4 * rows // m) == 0
    ]
    return max(fits)


def per_device(queries, key_rows, value_rows, out_grad, attn_out, log_norm, held_block, key_block):
    n_blk = lax.axis_size("blk")
    n = lax.axis_size("grp") * n_blk
    rows = queries.shape[0]
    m = relay_count(n, rows)
    part = 2 * KVH * rows // m
    lse = jnp.transpose(log_norm)
    vmem = pl.BlockSpec(memory_space=pltpu.VMEM)
    hbm = pl.BlockSpec(memory_space=pl.ANY)
    wide = pltpu.VMEM((rows, H * DH), jnp.bfloat16)
    line = pltpu.VMEM((H, 1, rows), jnp.float32)
    by_device = pltpu.VMEM((n, part, DH), jnp.bfloat16)
    by_slot = pltpu.VMEM((m, part, DH), jnp.bfloat16)
    acc = pltpu.VMEM((rows, DH), jnp.float32)
    small = pl.BlockSpec(memory_space=pltpu.SMEM)
    narrow = jax.ShapeDtypeStruct(key_rows.shape, jnp.bfloat16)
    return pl.pallas_call(
        functools.partial(fused_kernel, n, n_blk, m, 256),
        out_shape=(
            jax.ShapeDtypeStruct((rows, H * DH), jnp.bfloat16),
            narrow,
            narrow,
        ),
        in_specs=[small, small, vmem, vmem, vmem, hbm, hbm, hbm],
        out_specs=(hbm, vmem, vmem),
        scratch_shapes=[
            wide, wide, wide, wide, line, line,
            by_device, by_device, by_slot, by_slot, by_device,
            pltpu.VMEM((n, part, DH), jnp.float32), by_device,
            acc, acc, pltpu.SMEM((n,), jnp.int32), pltpu.SMEM((n,), jnp.int32),
            pltpu.SMEM((n,), jnp.int32), pltpu.SemaphoreType.DMA((12,)), pltpu.SemaphoreType.DMA((3,)),
        ],
        compiler_params=pltpu.CompilerParams(collective_id=0, has_side_effects=True),
    )(held_block, key_block, key_rows, value_rows, lse, queries, out_grad, attn_out)


def solution(mesh):
    row = jax.sharding.PartitionSpec(("grp", "blk"), None)
    flat = jax.sharding.PartitionSpec()
    return jax.shard_map(
        per_device,
        mesh=mesh,
        in_specs=(row, row, row, row, row, row, flat, flat),
        out_specs=(row, row, row),
        check_vma=False,
    )
```

```python
import functools

import jax
import jax.numpy as jnp
from jax import lax
from jax.experimental import pallas as pl
from jax.experimental.pallas import tpu as pltpu

H = 16
KVH = 2
DH = 128
GROUP = H // KVH
SCALE = DH ** (-0.5)
LOG2E = 1.4426950408889634
MESH = pl.DeviceIdType.MESH


def chunks_of(rows, width):
    return [(at, min(width, rows - at)) for at in range(0, rows, width)]


def own_place():
    return lax.axis_index("grp") * lax.axis_size("blk") + lax.axis_index("blk")


NT = (((1,), (1,)), ((), ()))
TN = (((0,), (0,)), ((), ()))
FAR = 1e30


def fused_kernel(
    n, n_blk, m, width, held_ref, key_ref, k_ref, v_ref, lse_ref, q_hbm, do_hbm, o_hbm,
    dq_hbm, dk_ref, dv_ref,
    q_ref, do_ref, o_ref, dq_ref, lse3, delta3, held, picked, kv, pair, terms, sums, sent,
    dk_acc, dv_acc, holder, before, last_of, sems, local_sems,
):
    rows = q_ref.shape[0]
    half = m // 2
    me = own_place()
    kind = lax.rem(me, 2)
    slot = kind * half + me // 2
    part = held.shape[1]
    block_row = pl.multiple_of(lax.rem(me // 2, half // 2) * part, part)
    of_keys = me // 2 < half // 2
    relay = me < m
    fetch_in, fetch_out, return_in, return_out = [sems.at[i] for i in range(4)]
    kv_out, kv_in, pair_out, grad_in = [(sems.at[i], sems.at[i + 1]) for i in range(4, 12, 2)]
    place = lambda t: (t // n_blk, lax.rem(t, n_blk))

    loads = [
        pltpu.make_async_copy(src, dst, local_sems.at[i])
        for i, (src, dst) in enumerate(((do_hbm, do_ref), (o_hbm, o_ref), (q_hbm, q_ref)))
    ]
    barrier = pltpu.get_barrier_semaphore()

    def greet(k, c):
        pl.semaphore_signal(
            barrier, inc=1, device_id=place(lax.rem(me + k, n)), device_id_type=MESH
        )
        return c

    lax.fori_loop(1, n, greet, 0)
    for load in loads:
        load.start()
    pl.semaphore_wait(barrier, n - 1)

    def to_relays(c, src, dst, send_sem, recv_sem):
        def push(k, carry):
            at = lax.rem(me // 2 + k, half)
            t = 2 * at + c

            @pl.when(t != me)
            def _():
                pltpu.make_async_remote_copy(
                    src_ref=src.at[c * half + at], dst_ref=dst.at[me],
                    send_sem=send_sem, recv_sem=recv_sem,
                    device_id=place(t), device_id_type=MESH,
                ).start()

            return carry

        lax.fori_loop(0, half, push, 0)

        @pl.when(jnp.logical_and(relay, kind == c))
        def _():
            dst[me] = src[slot]

    def send_blocks(c):
        cols = slice(c * DH, (c + 1) * DH)

        def push(k, carry):
            i = lax.rem(me // 2 + k, half // 2)
            row = pl.multiple_of(i * part, part)
            for src, at in ((k_ref, i), (v_ref, half // 2 + i)):
                t = 2 * at + c

                @pl.when(t != me)
                def _():
                    pltpu.make_async_remote_copy(
                        src_ref=src.at[pl.ds(row, part), cols], dst_ref=held.at[me],
                        send_sem=kv_out[c], recv_sem=fetch_in,
                        device_id=place(t), device_id_type=MESH,
                    ).start()

            return carry

        lax.fori_loop(0, half // 2, push, 0)
        mine = jnp.logical_and(relay, kind == c)

        @pl.when(jnp.logical_and(mine, of_keys))
        def _():
            held[me] = k_ref[pl.ds(block_row, part), cols]

        @pl.when(jnp.logical_and(mine, jnp.logical_not(of_keys)))
        def _():
            held[me] = v_ref[pl.ds(block_row, part), cols]

    def from_relay(src, dst, send_sem, recv_sem):
        def push(k, carry):
            t = lax.rem(me + k, n)
            pltpu.make_async_remote_copy(
                src_ref=src.at[t], dst_ref=dst,
                send_sem=send_sem, recv_sem=recv_sem,
                device_id=place(t), device_id_type=MESH,
            ).start()
            return carry

        lax.fori_loop(1, n, push, 0)

    def wait(ref, count, sem):
        part = ref.at[pl.ds(0, count)]
        pltpu.make_async_copy(part, part, sem).wait()

    def wait_pieces(c, ref, sem):
        mine = jnp.logical_and(relay, kind == c)

        @pl.when(mine)
        def _():
            wait(ref, half - 1, sem)

        @pl.when(jnp.logical_not(mine))
        def _():
            wait(ref, half, sem)

    def on_relay(c, work):
        @pl.when(jnp.logical_and(relay, kind == c))
        def _():
            work(c)

    def deliver(c):
        wait(held, n - 1, fetch_in)

        def pick(d, carry):
            picked[d] = held[holder[d]]
            return carry

        lax.fori_loop(0, n, pick, 0)
        from_relay(picked, kv.at[slot], fetch_out, kv_in[c])
        kv[slot] = picked[me]

    def settle(c):
        wait(terms, n - 1, return_in)

        def add(d, carry):
            earlier = before[d]
            total = jnp.where(earlier >= 0, sums[jnp.maximum(earlier, 0)], 0.0)
            sums[d] = total + terms[d].astype(jnp.float32)
            return carry

        sums[0] = jnp.zeros_like(sums[0])
        lax.fori_loop(0, n, add, 0)

        def pick(e, carry):
            d = last_of[e]
            total = jnp.where(d >= 0, sums[jnp.maximum(d, 0)], 0.0)
            sent[e] = total.astype(jnp.bfloat16)
            return carry

        lax.fori_loop(0, n, pick, 0)
        cols = slice(c * DH, (c + 1) * DH)
        for dst, mine in ((dk_ref, of_keys), (dv_ref, jnp.logical_not(of_keys))):

            @pl.when(mine)
            def _():
                spot = dst.at[pl.ds(block_row, part), cols]
                from_relay(sent, spot, return_out, grad_in[c])
                dst[pl.ds(block_row, part), cols] = sent[me]

    def heads(c, first, last):
        diag = jnp.where(held_ref[me] == key_ref[me], 1, 0)
        slack = rows * (1 - diag)

        def one(h, carry):
            col = pl.ds(pl.multiple_of(h * DH, DH), DH)
            k = kv[c * half : c * half + half // 2].reshape(rows, DH)
            v = kv[c * half + half // 2 : (c + 1) * half].reshape(rows, DH)
            dk, dv = dk_acc[...], dv_acc[...]
            for at, w in chunks_of(rows, width):
                q = q_ref[at : at + w, col]
                do = do_ref[at : at + w, col]
                lse = lse3[h, :, at : at + w]
                delta = delta3[h, :, at : at + w]
                s = lax.dot_general(k, q, NT, preferred_element_type=jnp.float32)
                s = s * (SCALE * LOG2E)
                i = lax.broadcasted_iota(jnp.int32, lse.shape, 1) + (at + slack)
                parts = []
                for low, size in chunks_of(rows, DH):
                    line = jnp.where(i < low, FAR, lse)
                    block = jnp.exp2(s[low : low + size] - line)
                    if at <= low < at + w:
                        left = low - at
                        square = block[:, left : left + size]
                        below = lax.broadcasted_iota(jnp.int32, square.shape, 0)
                        right = lax.broadcasted_iota(jnp.int32, square.shape, 1)
                        square = jnp.where(below - right <= slack, square, 0.0)
                        pieces = [block[:, :left], square, block[:, left + size :]]
                        block = jnp.concatenate([x for x in pieces if x.shape[1]], axis=1)
                    parts.append(block)
                p = jnp.concatenate(parts, axis=0)
                dp = lax.dot_general(v, do, NT, preferred_element_type=jnp.float32)
                ds = (p * (dp - delta)).astype(jnp.bfloat16)
                dv = dv + jnp.dot(p.astype(jnp.bfloat16), do, preferred_element_type=jnp.float32)
                dk = dk + jnp.dot(ds, q, preferred_element_type=jnp.float32)
                dq = lax.dot_general(ds, k, TN, preferred_element_type=jnp.float32)
                dq_ref[at : at + w, col] = (dq * SCALE).astype(jnp.bfloat16)
            dk_acc[...] = dk
            dv_acc[...] = dv
            return carry

        lax.fori_loop(first, last, one, 0)

    def clear():
        dk_acc[...] = jnp.zeros_like(dk_acc)
        dv_acc[...] = jnp.zeros_like(dv_acc)

    def store_pair(c):
        shape = (half // 2,) + pair.shape[1:]
        pair[c * half : c * half + half // 2] = (
            (dk_acc[...] * SCALE).astype(jnp.bfloat16).reshape(shape)
        )
        pair[c * half + half // 2 : (c + 1) * half] = (
            dv_acc[...].astype(jnp.bfloat16).reshape(shape)
        )

    send_blocks(0)

    def find(count, test, none):
        def step(i, found):
            return jnp.where(test(i), i, found)

        return lax.fori_loop(0, count, step, none, unroll=8)

    def plan_holder(d, carry):
        block = key_ref[d]
        holder[d] = find(n, lambda e: held_ref[e] == block, 0)
        return carry

    def plan_sums(d, carry):
        own = holder[d]
        before[d] = find(n, lambda i: jnp.logical_and(holder[i] == own, i < d), -1)
        last_of[d] = find(n, lambda i: holder[i] == d, -1)
        return carry

    lax.fori_loop(0, n, plan_holder, 0)
    lax.fori_loop(0, n, plan_sums, 0)
    for h in range(H):
        lse3[h] = lse_ref[h : h + 1, :] * LOG2E
    loads[0].wait()
    loads[1].wait()

    def make_delta(h, carry):
        col = pl.ds(pl.multiple_of(h * DH, DH), DH)
        prod = do_ref[:, col].astype(jnp.float32) * o_ref[:, col].astype(jnp.float32)
        delta3[h] = jnp.sum(jnp.transpose(prod), axis=0, keepdims=True)
        return carry

    lax.fori_loop(0, H, make_delta, 0)
    loads[2].wait()
    first = jnp.logical_and(relay, kind == 0)

    @pl.when(first)
    def _():
        deliver(0)
        send_blocks(1)

    wait_pieces(0, kv, kv_in[0])

    @pl.when(jnp.logical_not(first))
    def _():
        send_blocks(1)

    clear()
    heads(0, 0, GROUP // 2)
    on_relay(1, deliver)
    heads(0, GROUP // 2, GROUP)
    store_pair(0)
    to_relays(0, pair, terms, pair_out[0], return_in)
    wait_pieces(1, kv, kv_in[1])
    clear()
    heads(1, GROUP, GROUP + GROUP // 2)
    on_relay(0, settle)
    heads(1, GROUP + GROUP // 2, H)
    store_pair(1)
    to_relays(1, pair, terms, pair_out[1], return_in)
    save = pltpu.make_async_copy(dq_ref, dq_hbm, local_sems.at[0])
    save.start()
    on_relay(1, settle)
    for c in range(KVH):
        wait_pieces(c, kv, kv_out[c])
        wait_pieces(c, pair, pair_out[c])
        wait_pieces(c, pair, grad_in[c])

    @pl.when(relay)
    def _():
        wait(picked, n - 1, fetch_out)
        wait(sent, n - 1, return_out)

    save.wait()


def relay_count(n, rows):
    fits = [
        m for m in range(4, n + 1, 4)
        if 4 * rows % m == 0 and (4 * rows // m) % 16 == 0 and rows % (4 * rows // m) == 0
    ]
    return max(fits)


def per_device(queries, key_rows, value_rows, out_grad, attn_out, log_norm, held_block, key_block):
    n_blk = lax.axis_size("blk")
    n = lax.axis_size("grp") * n_blk
    rows = queries.shape[0]
    m = relay_count(n, rows)
    part = 2 * KVH * rows // m
    lse = jnp.transpose(log_norm)
    vmem = pl.BlockSpec(memory_space=pltpu.VMEM)
    hbm = pl.BlockSpec(memory_space=pl.ANY)
    wide = pltpu.VMEM((rows, H * DH), jnp.bfloat16)
    line = pltpu.VMEM((H, 1, rows), jnp.float32)
    by_device = pltpu.VMEM((n, part, DH), jnp.bfloat16)
    by_slot = pltpu.VMEM((m, part, DH), jnp.bfloat16)
    acc = pltpu.VMEM((rows, DH), jnp.float32)
    small = pl.BlockSpec(memory_space=pltpu.SMEM)
    narrow = jax.ShapeDtypeStruct(key_rows.shape, jnp.bfloat16)
    return pl.pallas_call(
        functools.partial(fused_kernel, n, n_blk, m, rows),
        out_shape=(
            jax.ShapeDtypeStruct((rows, H * DH), jnp.bfloat16),
            narrow,
            narrow,
        ),
        in_specs=[small, small, vmem, vmem, vmem, hbm, hbm, hbm],
        out_specs=(hbm, vmem, vmem),
        scratch_shapes=[
            wide, wide, wide, wide, line, line,
            by_device, by_device, by_slot, by_slot, by_device,
            pltpu.VMEM((n, part, DH), jnp.float32), by_device,
            acc, acc, pltpu.SMEM((n,), jnp.int32), pltpu.SMEM((n,), jnp.int32),
            pltpu.SMEM((n,), jnp.int32), pltpu.SemaphoreType.DMA((12,)), pltpu.SemaphoreType.DMA((3,)),
        ],
        compiler_params=pltpu.CompilerParams(collective_id=0, has_side_effects=True),
    )(held_block, key_block, key_rows, value_rows, lse, queries, out_grad, attn_out)


def solution(mesh):
    row = jax.sharding.PartitionSpec(("grp", "blk"), None)
    flat = jax.sharding.PartitionSpec()
    return jax.shard_map(
        per_device,
        mesh=mesh,
        in_specs=(row, row, row, row, row, row, flat, flat),
        out_specs=(row, row, row),
        check_vma=False,
    )
```

```python
import functools

import jax
import jax.numpy as jnp
from jax import lax
from jax.experimental import pallas as pl
from jax.experimental.pallas import tpu as pltpu

H = 16
KVH = 2
DH = 128
GROUP = H // KVH
SCALE = DH ** (-0.5)
LOG2E = 1.4426950408889634
MESH = pl.DeviceIdType.MESH


def chunks_of(rows, width):
    return [(at, min(width, rows - at)) for at in range(0, rows, width)]


def own_place():
    return lax.axis_index("grp") * lax.axis_size("blk") + lax.axis_index("blk")


NT = (((1,), (1,)), ((), ()))
TN = (((0,), (0,)), ((), ()))
FAR = 1e30


def fused_kernel(
    n, n_blk, m, width, held_ref, key_ref, k_ref, v_ref, lse_ref, q_hbm, do_hbm, o_hbm,
    dq_hbm, dk_ref, dv_ref,
    q_ref, do_ref, o_ref, dq_ref, lse3, delta3, held, picked, kv, pair, terms, sums, sent,
    dk_acc, dv_acc, holder, before, last_of, sems, local_sems,
):
    rows = q_ref.shape[0]
    half = m // 2
    me = own_place()
    kind = lax.rem(me, 2)
    slot = kind * half + me // 2
    part = held.shape[1]
    block_row = pl.multiple_of(lax.rem(me // 2, half // 2) * part, part)
    of_keys = me // 2 < half // 2
    relay = me < m
    fetch_in, fetch_out, return_in, return_out = [sems.at[i] for i in range(4)]
    kv_out, kv_in, pair_out, grad_in = [(sems.at[i], sems.at[i + 1]) for i in range(4, 12, 2)]
    place = lambda t: (t // n_blk, lax.rem(t, n_blk))

    loads = [
        pltpu.make_async_copy(src, dst, local_sems.at[i])
        for i, (src, dst) in enumerate(((do_hbm, do_ref), (o_hbm, o_ref), (q_hbm, q_ref)))
    ]
    barrier = pltpu.get_barrier_semaphore()

    def greet(k, c):
        pl.semaphore_signal(
            barrier, inc=1, device_id=place(lax.rem(me + k, n)), device_id_type=MESH
        )
        return c

    lax.fori_loop(1, n, greet, 0)
    for load in loads:
        load.start()
    pl.semaphore_wait(barrier, n - 1)

    def to_relays(c, src, dst, send_sem, recv_sem):
        def push(k, carry):
            at = lax.rem(me // 2 + k, half)
            t = 2 * at + c

            @pl.when(t != me)
            def _():
                pltpu.make_async_remote_copy(
                    src_ref=src.at[c * half + at], dst_ref=dst.at[me],
                    send_sem=send_sem, recv_sem=recv_sem,
                    device_id=place(t), device_id_type=MESH,
                ).start()

            return carry

        lax.fori_loop(0, half, push, 0)

        @pl.when(jnp.logical_and(relay, kind == c))
        def _():
            dst[me] = src[slot]

    def send_blocks(c):
        cols = slice(c * DH, (c + 1) * DH)

        def push(k, carry):
            i = lax.rem(me // 2 + k, half // 2)
            row = pl.multiple_of(i * part, part)
            for src, at in ((k_ref, i), (v_ref, half // 2 + i)):
                t = 2 * at + c

                @pl.when(t != me)
                def _():
                    pltpu.make_async_remote_copy(
                        src_ref=src.at[pl.ds(row, part), cols], dst_ref=held.at[me],
                        send_sem=kv_out[c], recv_sem=fetch_in,
                        device_id=place(t), device_id_type=MESH,
                    ).start()

            return carry

        lax.fori_loop(0, half // 2, push, 0)
        mine = jnp.logical_and(relay, kind == c)

        @pl.when(jnp.logical_and(mine, of_keys))
        def _():
            held[me] = k_ref[pl.ds(block_row, part), cols]

        @pl.when(jnp.logical_and(mine, jnp.logical_not(of_keys)))
        def _():
            held[me] = v_ref[pl.ds(block_row, part), cols]

    def from_relay(src, dst, send_sem, recv_sem):
        def push(k, carry):
            t = lax.rem(me + k, n)
            pltpu.make_async_remote_copy(
                src_ref=src.at[t], dst_ref=dst,
                send_sem=send_sem, recv_sem=recv_sem,
                device_id=place(t), device_id_type=MESH,
            ).start()
            return carry

        lax.fori_loop(1, n, push, 0)

    def wait(ref, count, sem):
        part = ref.at[pl.ds(0, count)]
        pltpu.make_async_copy(part, part, sem).wait()

    def wait_pieces(c, ref, sem):
        mine = jnp.logical_and(relay, kind == c)

        @pl.when(mine)
        def _():
            wait(ref, half - 1, sem)

        @pl.when(jnp.logical_not(mine))
        def _():
            wait(ref, half, sem)

    def on_relay(c, work):
        @pl.when(jnp.logical_and(relay, kind == c))
        def _():
            work(c)

    def deliver(c):
        wait(held, n - 1, fetch_in)

        def pick(d, carry):
            picked[d] = held[holder[d]]
            return carry

        lax.fori_loop(0, n, pick, 0)
        from_relay(picked, kv.at[slot], fetch_out, kv_in[c])
        kv[slot] = picked[me]

    def settle(c):
        wait(terms, n - 1, return_in)

        def add(d, carry):
            earlier = before[d]
            total = jnp.where(earlier >= 0, sums[jnp.maximum(earlier, 0)], 0.0)
            sums[d] = total + terms[d].astype(jnp.float32)
            return carry

        sums[0] = jnp.zeros_like(sums[0])
        lax.fori_loop(0, n, add, 0)

        def pick(e, carry):
            d = last_of[e]
            total = jnp.where(d >= 0, sums[jnp.maximum(d, 0)], 0.0)
            sent[e] = total.astype(jnp.bfloat16)
            return carry

        lax.fori_loop(0, n, pick, 0)
        cols = slice(c * DH, (c + 1) * DH)
        for dst, mine in ((dk_ref, of_keys), (dv_ref, jnp.logical_not(of_keys))):

            @pl.when(mine)
            def _():
                spot = dst.at[pl.ds(block_row, part), cols]
                from_relay(sent, spot, return_out, grad_in[c])
                dst[pl.ds(block_row, part), cols] = sent[me]

    def heads(c, first, last):
        diag = jnp.where(held_ref[me] == key_ref[me], 1, 0)
        slack = rows * (1 - diag)

        def one(h, carry):
            col = pl.ds(pl.multiple_of(h * DH, DH), DH)
            k = kv[c * half : c * half + half // 2].reshape(rows, DH)
            v = kv[c * half + half // 2 : (c + 1) * half].reshape(rows, DH)
            dk, dv = dk_acc[...], dv_acc[...]
            for at, w in chunks_of(rows, width):
                q = q_ref[at : at + w, col]
                do = do_ref[at : at + w, col]
                lse = lse3[h, :, at : at + w]
                delta = delta3[h, :, at : at + w]
                s = lax.dot_general(k, q, NT, preferred_element_type=jnp.float32)
                s = s * (SCALE * LOG2E)
                i = lax.broadcasted_iota(jnp.int32, lse.shape, 1) + (at + slack)
                parts = []
                for low, size in chunks_of(rows, DH):
                    line = jnp.where(i < low, FAR, lse)
                    block = jnp.exp2(s[low : low + size] - line)
                    if at <= low < at + w:
                        left = low - at
                        square = block[:, left : left + size]
                        below = lax.broadcasted_iota(jnp.int32, square.shape, 0)
                        right = lax.broadcasted_iota(jnp.int32, square.shape, 1)
                        square = jnp.where(below - right <= slack, square, 0.0)
                        pieces = [block[:, :left], square, block[:, left + size :]]
                        block = jnp.concatenate([x for x in pieces if x.shape[1]], axis=1)
                    parts.append(block)
                p = jnp.concatenate(parts, axis=0)
                dp = lax.dot_general(v, do, NT, preferred_element_type=jnp.float32)
                ds = (p * (dp - delta)).astype(jnp.bfloat16)
                dv = dv + jnp.dot(p.astype(jnp.bfloat16), do, preferred_element_type=jnp.float32)
                dk = dk + jnp.dot(ds, q, preferred_element_type=jnp.float32)
                dq = lax.dot_general(ds, k, TN, preferred_element_type=jnp.float32)
                dq_ref[at : at + w, col] = (dq * SCALE).astype(jnp.bfloat16)
            dk_acc[...] = dk
            dv_acc[...] = dv
            return carry

        lax.fori_loop(first, last, one, 0)

    def clear():
        dk_acc[...] = jnp.zeros_like(dk_acc)
        dv_acc[...] = jnp.zeros_like(dv_acc)

    def store_pair(c):
        shape = (half // 2,) + pair.shape[1:]
        pair[c * half : c * half + half // 2] = (
            (dk_acc[...] * SCALE).astype(jnp.bfloat16).reshape(shape)
        )
        pair[c * half + half // 2 : (c + 1) * half] = (
            dv_acc[...].astype(jnp.bfloat16).reshape(shape)
        )

    send_blocks(0)

    def find(count, test, none):
        def step(i, found):
            return jnp.where(test(i), i, found)

        return lax.fori_loop(0, count, step, none, unroll=8)

    def plan_holder(d, carry):
        block = key_ref[d]
        holder[d] = find(n, lambda e: held_ref[e] == block, 0)
        return carry

    def plan_sums(d, carry):
        own = holder[d]
        before[d] = find(n, lambda i: jnp.logical_and(holder[i] == own, i < d), -1)
        last_of[d] = find(n, lambda i: holder[i] == d, -1)
        return carry

    lax.fori_loop(0, n, plan_holder, 0)
    lax.fori_loop(0, n, plan_sums, 0)
    for h in range(H):
        lse3[h] = lse_ref[h : h + 1, :] * LOG2E
    loads[0].wait()
    loads[1].wait()

    def make_delta(h, carry):
        col = pl.ds(pl.multiple_of(h * DH, DH), DH)
        prod = do_ref[:, col].astype(jnp.float32) * o_ref[:, col].astype(jnp.float32)
        delta3[h] = jnp.sum(jnp.transpose(prod), axis=0, keepdims=True)
        return carry

    lax.fori_loop(0, H, make_delta, 0)
    loads[2].wait()
    first = jnp.logical_and(relay, kind == 0)

    @pl.when(first)
    def _():
        deliver(0)
        send_blocks(1)

    @pl.when(jnp.logical_not(first))
    def _():
        send_blocks(1)

    wait_pieces(0, kv, kv_in[0])
    clear()
    heads(0, 0, GROUP // 2)
    on_relay(1, deliver)
    heads(0, GROUP // 2, GROUP)
    store_pair(0)
    to_relays(0, pair, terms, pair_out[0], return_in)
    wait_pieces(1, kv, kv_in[1])
    clear()
    heads(1, GROUP, GROUP + GROUP // 2)
    on_relay(0, settle)
    heads(1, GROUP + GROUP // 2, H)
    store_pair(1)
    to_relays(1, pair, terms, pair_out[1], return_in)
    save = pltpu.make_async_copy(dq_ref, dq_hbm, local_sems.at[0])
    save.start()
    on_relay(1, settle)
    for c in range(KVH):
        wait_pieces(c, kv, kv_out[c])
        wait_pieces(c, pair, pair_out[c])
        wait_pieces(c, pair, grad_in[c])

    @pl.when(relay)
    def _():
        wait(picked, n - 1, fetch_out)
        wait(sent, n - 1, return_out)

    save.wait()


def relay_count(n, rows):
    fits = [
        m for m in range(4, n + 1, 4)
        if 4 * rows % m == 0 and (4 * rows // m) % 16 == 0 and rows % (4 * rows // m) == 0
    ]
    return max(fits)


def per_device(queries, key_rows, value_rows, out_grad, attn_out, log_norm, held_block, key_block):
    n_blk = lax.axis_size("blk")
    n = lax.axis_size("grp") * n_blk
    rows = queries.shape[0]
    m = relay_count(n, rows)
    part = 2 * KVH * rows // m
    lse = jnp.transpose(log_norm)
    vmem = pl.BlockSpec(memory_space=pltpu.VMEM)
    hbm = pl.BlockSpec(memory_space=pl.ANY)
    wide = pltpu.VMEM((rows, H * DH), jnp.bfloat16)
    line = pltpu.VMEM((H, 1, rows), jnp.float32)
    by_device = pltpu.VMEM((n, part, DH), jnp.bfloat16)
    by_slot = pltpu.VMEM((m, part, DH), jnp.bfloat16)
    acc = pltpu.VMEM((rows, DH), jnp.float32)
    small = pl.BlockSpec(memory_space=pltpu.SMEM)
    narrow = jax.ShapeDtypeStruct(key_rows.shape, jnp.bfloat16)
    return pl.pallas_call(
        functools.partial(fused_kernel, n, n_blk, m, rows),
        out_shape=(
            jax.ShapeDtypeStruct((rows, H * DH), jnp.bfloat16),
            narrow,
            narrow,
        ),
        in_specs=[small, small, vmem, vmem, vmem, hbm, hbm, hbm],
        out_specs=(hbm, vmem, vmem),
        scratch_shapes=[
            wide, wide, wide, wide, line, line,
            by_device, by_device, by_slot, by_slot, by_device,
            pltpu.VMEM((n, part, DH), jnp.float32), by_device,
            acc, acc, pltpu.SMEM((n,), jnp.int32), pltpu.SMEM((n,), jnp.int32),
            pltpu.SMEM((n,), jnp.int32), pltpu.SemaphoreType.DMA((12,)), pltpu.SemaphoreType.DMA((3,)),
        ],
        compiler_params=pltpu.CompilerParams(collective_id=0, has_side_effects=True),
    )(held_block, key_block, key_rows, value_rows, lse, queries, out_grad, attn_out)


def solution(mesh):
    row = jax.sharding.PartitionSpec(("grp", "blk"), None)
    flat = jax.sharding.PartitionSpec()
    return jax.shard_map(
        per_device,
        mesh=mesh,
        in_specs=(row, row, row, row, row, row, flat, flat),
        out_specs=(row, row, row),
        check_vma=False,
    )
```
